512 devices in a mesh: occ: 64 (over y, z), vir: 8 (over x, core).
Axes of the slice: x: 4, y: 4, z: 16, core: 2. Of those that a mesh axis runs over, the one named last changes fastest.
Arguments:
- t2_tiles: bfloat16 [16384, 128, 128], P(('occ', 'vir')), may hold values from -6 to 6
- tile_owner: int32 [16384, 1], P(('occ', 'vir')), may hold values from 0 to 63; in each aligned block of 32 rows (0 to 31, 32 to 63, ...) at most 2 rows name the same one
- tile_block: int32 [16384], P(('occ', 'vir')), may hold values from 0 to 1
- tile_cd: int32 [16384], P(('occ', 'vir')), may hold values from 0 to 3
- ladder_ints: bfloat16 [4096, 2048], P('vir', 'occ'), may hold values from -0.75 to 0.75
- cycle_amps: bfloat16 [16384, 1024], P('occ', 'vir'), may hold values from -6 to 6
- cycle_ints: bfloat16 [1024, 2048], P('vir'), may hold values from -0.25 to 0.25
Outputs:
- residual: bfloat16 [16384, 2048], P('occ', 'vir')
The draws below stay inside these ranges and needn't reach their ends.
Inputs may be any that keep to these rules, and one draw needn't show every extreme that they name: `tile_owner`: among the tiles of one device (aligned blocks of 32 tiles), no owner is named more than 2 times, a bound that some block reaches.
All inputs are finite; a program needn't handle non-finite values.
Results may differ from the reference program's by a relative error of at most 0.0048.
Values may be sent and summed in bfloat16 or wider, within the bound.
A program may use at most 64 MiB of HBM per device.

```python
import math
import jax
import jax.numpy as jnp
import numpy as np

TILE = 128
NT_DEV = 32
BLK_DEV = 2
CD_DEV = 4
CAP = 2
TILES = 16384
ROWS = 16384
CD_ALL = 4096
AB_ALL = 2048
RK_ALL = 1024
N_OCC = 64
N_VIR = 8


def plant(array, stream_key, least, high):
    index_at = [jax.random.randint(jax.random.fold_in(stream_key, axis), (), 0, length) for axis, length in enumerate(array.shape)]
    main_axis = array.shape.index(max(array.shape))
    next_to = index_at[:main_axis] + [(index_at[main_axis] + 1) % array.shape[main_axis]] + index_at[main_axis + 1:]
    return array.at[tuple(index_at)].set(least).at[tuple(next_to)].set(high)


def raised(values, rng, source, target, shards_of, factor):
    owner, partner = [(jnp.arange(values.shape[dim]) // (values.shape[dim] // shards_of)).reshape([-1 if axis == dim else 1 for axis in range(values.ndim)]) for dim in (source, target)]
    chosen = jax.random.permutation(rng, shards_of)[partner]
    strong = (owner == chosen) | (owner == (partner + shards_of // 2) % shards_of)
    return jnp.where(strong, factor * values, values)


def block_levels(rng, dims, shards, smallest, high):
    def one(position, blocks):
        steps = jax.random.uniform(jax.random.fold_in(jax.random.fold_in(rng, 6), position), (blocks,), jnp.float32, smallest / len(shards), high / len(shards))
        return jnp.repeat(jnp.exp(steps), dims[position] // blocks).reshape((-1,) + (1,) * (len(dims) - position - 1))

    factor_of = one(*shards[0])
    for cut in shards[1:]:
        factor_of = factor_of * one(*cut)
    return factor_of


def shared_out(stream_key, own, number, rows, amount, top, most, lean):
    sequence = jax.random.permutation(stream_key, amount)
    heavy_load, usual = portions_of(amount, rows * top, most, lean, True), portions_of(amount, rows * top, most, lean, False)
    places = jnp.arange(amount)

    def named(tallies, turn):
        used = int((tallies > 0).sum())
        fixed = max(1, used // 4)
        passed = fixed + (places - fixed + turn * (used - fixed)) % max(1, amount - fixed)
        return jnp.zeros((amount,), jnp.int32).at[sequence[jnp.where(places < fixed, places, passed)]].set(jnp.asarray(tallies, jnp.int32))

    tallies = jnp.where(number % 4 == 0, named(heavy_load, number // 4), named(usual, number - number // 4 - 1))
    mixed = jax.random.permutation(jax.random.fold_in(own, 3), amount)
    donor, receiver = mixed[0:amount // 2 * 2:2], mixed[1:amount // 2 * 2:2]
    slack = jnp.minimum(tallies[donor] - 1, most - tallies[receiver]) // 2
    slack = jnp.where((donor == sequence[0]) | (receiver == sequence[0]) | (tallies[receiver] == 0), 0, jnp.maximum(slack, 0))
    passed = jax.random.randint(jax.random.fold_in(own, 4), (amount // 2,), 0, 1 << 20) % (slack + 1)
    tallies = tallies.at[donor].add(-passed).at[receiver].add(passed)
    members = jnp.searchsorted(jnp.cumsum(tallies), jnp.arange(rows * top), side="right").astype(jnp.int32)
    listing = members.reshape(top, rows).T
    listing = listing[jax.random.permutation(jax.random.fold_in(own, 1), rows)]
    turn = jax.random.randint(jax.random.fold_in(own, 2), (rows, 1), 0, top)
    return jnp.take_along_axis(listing, (jnp.arange(top)[None, :] + turn) % top, axis=1)


def portions_of(count, total, most, lean, full):
    loads = [(1 << 20) // math.isqrt(standing ** lean) + 1 for standing in range(1, count + 1)]
    largest = most if full else min(most, max(-(-total // count), total * loads[0] // sum(loads)))
    least = 1 if total - largest >= count - 1 else 0
    given, spare = [largest] + [least] * (count - 1), total - largest - least * (count - 1)
    while spare > 0:
        movable = [i for i in range(1, count) if given[i] < largest] or [i for i in range(1, count) if given[i] < most]
        pool, left = sum([loads[i] for i in movable]), spare
        for i in movable:
            more = min(most - given[i], max(1, left * loads[i] // pool), spare)
            given[i] = given[i] + more
            spare = spare - more
    return np.array(given)


def noise(rng, extent, width, reach, split=(), kind=jnp.bfloat16):
    level = block_levels(rng, extent, split, -0.22, 0.18) if split else 1.0
    entries = jax.random.normal(rng, extent, jnp.float32) * width * level
    return jnp.minimum(jnp.maximum(entries, -reach), reach).astype(kind)


def heavy_noise(rng, extent, deviation, most, shards, heavy, kind=jnp.bfloat16):
    entries = deviation * jax.random.normal(rng, extent, jnp.float32)
    if shards:
        entries = entries * block_levels(rng, extent, shards, -0.22, 0.18)
    return jnp.clip(raised(entries, jax.random.fold_in(rng, 3), *heavy), -most, most).astype(kind)


def setup_inputs(seed: int = 0) -> dict:
    key_list = jax.random.split(jax.random.key(seed), 8)
    t2_tiles = noise(key_list[0], (TILES, TILE, TILE), 1.0, 6.0, ((0, 512),))
    tile_owner_keys = jax.random.split(jax.random.fold_in(key_list[1], 1), TILES // NT_DEV)
    tile_owner_turns = jax.random.permutation(jax.random.fold_in(key_list[1], 3), TILES // NT_DEV)
    tile_owner = jax.vmap(lambda own, number: shared_out(jax.random.fold_in(key_list[1], 2), own, number, NT_DEV, N_OCC, 1, CAP, 2))(tile_owner_keys, tile_owner_turns).reshape((TILES, 1))
    tile_block = plant(jax.random.randint(key_list[2], (TILES,), 0, BLK_DEV), jax.random.fold_in(key_list[2], 1), 0, BLK_DEV - 1).astype(jnp.int32)
    tile_cd = plant(jax.random.randint(key_list[3], (TILES,), 0, CD_DEV), jax.random.fold_in(key_list[3], 1), 0, CD_DEV - 1).astype(jnp.int32)
    ladder_ints = heavy_noise(key_list[4], (CD_ALL, AB_ALL), (CD_DEV * TILE) ** -0.5, 0.75, ((0, 8), (1, 64)), (0, 1, 64, 4.0))
    cycle_amps = noise(key_list[5], (ROWS, RK_ALL), 1.0, 6.0, ((0, 64), (1, 8)))
    cycle_ints = heavy_noise(key_list[6], (RK_ALL, AB_ALL), RK_ALL ** -0.5, 0.25, ((0, 8),), (0, 1, 8, 2.0))
    return dict(t2_tiles=t2_tiles, tile_owner=tile_owner, tile_block=tile_block, tile_cd=tile_cd, ladder_ints=ladder_ints, cycle_amps=cycle_amps, cycle_ints=cycle_ints)


def reference(t2_tiles, tile_owner, tile_block, tile_cd, ladder_ints, cycle_amps, cycle_ints):
    tiles = t2_tiles.reshape(N_OCC, N_VIR, NT_DEV, TILE, TILE)
    owners = tile_owner.reshape(N_OCC, N_VIR, NT_DEV)
    blocks = tile_block.reshape(N_OCC, N_VIR, NT_DEV)
    columns = tile_cd.reshape(N_OCC, N_VIR, NT_DEV)
    n_blocks = N_OCC * BLK_DEV
    combined = jnp.dot(cycle_amps, cycle_ints, preferred_element_type=jnp.float32)
    for column in range(N_VIR):
        segment = ((owners[:, column] * BLK_DEV + blocks[:, column]) * CD_DEV + columns[:, column]).reshape(-1).astype(jnp.int32)
        placed = jax.ops.segment_sum(tiles[:, column].reshape(-1, TILE, TILE).astype(jnp.float32), segment, num_segments=n_blocks * CD_DEV)
        amplitudes = placed.reshape(n_blocks, CD_DEV, TILE, TILE).transpose(0, 2, 1, 3).reshape(n_blocks * TILE, CD_DEV * TILE).astype(jnp.bfloat16)
        rows = ladder_ints[column * CD_DEV * TILE:(column + 1) * CD_DEV * TILE]
        combined = combined + jnp.dot(amplitudes, rows, preferred_element_type=jnp.float32)
    return combined.astype(jnp.bfloat16)
```

```python
import jax
import jax.numpy as jnp
from jax import lax
from jax.sharding import PartitionSpec as P

NY = 4


def body(t2_tiles, tile_owner, tile_block, tile_cd, ladder_ints, cycle_amps, cycle_ints):
    n_occ = lax.axis_size("occ")
    nz = n_occ // NY
    tile_count, tile_size = t2_tiles.shape[:2]
    pair_rows = cycle_amps.shape[0]
    blocks = pair_rows // tile_size
    cd_tiles = ladder_ints.shape[0] // tile_size
    combos = blocks * cd_tiles
    y_groups = [[y * nz + z for y in range(NY)] for z in range(nz)]
    z_groups = [[y * nz + z for z in range(nz)] for y in range(NY)]
    codes = tile_owner[:, 0] * combos + tile_block * cd_tiles + tile_cd
    got_tiles = lax.all_gather(
        t2_tiles.reshape(tile_count, tile_size * tile_size),
        "occ", axis=0, tiled=True, axis_index_groups=y_groups,
    )
    got_codes = lax.all_gather(codes, "occ", axis=0, tiled=True, axis_index_groups=y_groups)
    full_ladder = lax.all_gather(ladder_ints, "occ", axis=1, tiled=True)
    my_y = lax.axis_index("occ") // nz
    targets = my_y * (nz * combos) + jnp.arange(nz * combos, dtype=jnp.int32)
    select = (got_codes[:, None] == targets[None, :]).astype(jnp.bfloat16)
    summed = jnp.einsum("sc,sx->cx", select, got_tiles, preferred_element_type=jnp.float32)
    summed = lax.psum_scatter(
        summed.astype(jnp.bfloat16), "occ", scatter_dimension=0, tiled=True,
        axis_index_groups=z_groups,
    )
    amplitudes = (
        summed.reshape(blocks, cd_tiles, tile_size, tile_size)
        .transpose(0, 2, 1, 3)
        .reshape(pair_rows, cd_tiles * tile_size)
    )
    cycle_part = jnp.dot(cycle_amps, cycle_ints, preferred_element_type=jnp.float32)
    ladder = jnp.dot(amplitudes, full_ladder, preferred_element_type=jnp.float32)
    combined = ladder + cycle_part
    return lax.psum_scatter(combined, "vir", scatter_dimension=1, tiled=True).astype(jnp.bfloat16)


def solution(mesh):
    in_specs = (
        P(("occ", "vir"), None, None),
        P(("occ", "vir"), None),
        P(("occ", "vir")),
        P(("occ", "vir")),
        P("vir", "occ"),
        P("occ", "vir"),
        P("vir", None),
    )
    return jax.shard_map(
        body, mesh=mesh, in_specs=in_specs, out_specs=P("occ", "vir"), check_vma=False
    )
```

```python
import functools

import jax
import jax.numpy as jnp
from jax import lax
from jax.experimental import pallas as pl
from jax.experimental.pallas import tpu as pltpu
from jax.sharding import PartitionSpec as P

MESH = pl.DeviceIdType.MESH
NY = 4
NC = 4
LAG = 2
BF = jnp.bfloat16
F32 = jnp.float32


def kernel(
    t2_ref, code_ref, lad_ref, camp_ref, cint_ref, out_ref,
    gath, codes, sel, ysum, zin, lgat, part, acc, amps, pout, pin, xs, xh, xi,
    ysend, yrecv, csend, crecv, zsend, zrecv, lzs, lzr, lys, lyr, ps, pr, xsend, xrecv, local,
):
    nz = lgat.shape[1]
    rows = t2_ref.shape[0]
    cr = rows // NC
    half = cr // 2
    nx = pout.shape[0]
    occ, vir = lax.axis_index("occ"), lax.axis_index("vir")
    y, z = occ // nz, occ % nz
    x, core = vir // 2, vir % 2

    def at_y(d):
        return (y + d + NY) % NY

    def at_z(d):
        return (z + d + nz) % nz

    def at_x(d):
        return (x + d + nx) % nx

    def to_y(d):
        return {"occ": at_y(d) * nz + z}

    def to_z(d):
        return {"occ": y * nz + at_z(d)}

    def to_x(d):
        return {"vir": at_x(d) * 2 + core}

    partner = {"vir": x * 2 + (1 - core)}

    def remote(src, dst, send, recv, where):
        return pltpu.make_async_remote_copy(
            src_ref=src, dst_ref=dst, send_sem=send, recv_sem=recv, device_id=where,
            device_id_type=MESH,
        )

    def chunk(c):
        return pl.ds(c * cr, cr)

    def own_y(c, d):
        return remote(
            t2_ref.at[chunk(c)], gath.at[chunk(c), y], ysend.at[c, d], yrecv.at[c, d],
            to_y(1 - 2 * d),
        )

    def own_y_in(c, d):
        return remote(
            t2_ref.at[chunk(c)], gath.at[chunk(c), at_y(2 * d - 1)], ysend.at[c, d],
            yrecv.at[c, d], to_y(1 - 2 * d),
        )

    def piece(c, d):
        return pl.ds(c * cr + d * half, half)

    def fwd_y(c, d):
        block = gath.at[piece(c, d), at_y(2 * d - 1)]
        return remote(block, block, ysend.at[c, 2 + d], yrecv.at[c, 2 + d], to_y(1 - 2 * d))

    def fwd_y_in(c, d):
        block = gath.at[piece(c, d), at_y(2)]
        return remote(block, block, ysend.at[c, 2 + d], yrecv.at[c, 2 + d], to_y(1 - 2 * d))

    def code_out(d):
        return remote(code_ref, codes.at[y], csend.at[d - 1], crecv.at[d - 1], to_y(d))

    def code_in(d):
        return remote(code_ref, codes.at[at_y(-d)], csend.at[d - 1], crecv.at[d - 1], to_y(d))

    def arm(c, d):
        return nz // 2 if (c + d) % 2 == 0 else nz - 1 - nz // 2

    def z_copy(c, d, s):
        block = ysum.at[at_z((1 - 2 * d) * (arm(c, d) - s)), chunk(c)]
        return remote(
            block, zin.at[d, s, chunk(c)], zsend.at[c, d, s], zrecv.at[c, d, s], to_z(1 - 2 * d)
        )

    steps = (nz // 2, nz - 1 - nz // 2)

    def lad_z(d, s):
        block = lgat.at[y, at_z((2 * d - 1) * s)]
        src = lad_ref if s == 0 else block
        return remote(src, block, lzs.at[d, s], lzr.at[d, s], to_z(1 - 2 * d))

    def lad_z_in(d, s):
        block = lgat.at[y, at_z((2 * d - 1) * (s + 1))]
        return remote(block, block, lzs.at[d, s], lzr.at[d, s], to_z(1 - 2 * d))

    def lad_y(d, source):
        block = lgat.at[at_y(source)]
        return remote(block, block, lys.at[d], lyr.at[d], to_y(1 - 2 * d))

    def lad_fwd(d, source):
        block = lgat.at[at_y(source), pl.ds(d * (nz // 2), nz // 2)]
        return remote(block, block, lys.at[2 + d], lyr.at[2 + d], to_y(1 - 2 * d))

    barrier = pltpu.get_barrier_semaphore()
    peers = [to_y(1), to_y(2), to_y(-1), to_z(1), to_z(-1), to_x(1), to_x(-1), partner]
    for peer in peers:
        pl.semaphore_signal(barrier, inc=1, device_id=peer, device_id_type=MESH)
    pl.semaphore_wait(barrier, len(peers))

    for d in (1, 2, 3):
        code_out(d).start()
    for c in (0, 1):
        for d in (0, 1):
            own_y(c, d).start()
    mine_t2 = pltpu.make_async_copy(t2_ref, gath.at[:, y], local.at[0])
    mine_lad = pltpu.make_async_copy(lad_ref, lgat.at[y, z], local.at[1])
    mine_t2.start()
    mine_lad.start()

    def stage_a(c):
        for d in (0, 1):
            own_y_in(c, d).wait_recv()
            fwd_y(c, d).start()
        if c + 2 < NC:
            for d in (0, 1):
                own_y(c + 2, d).start()

    def lad_step(s):
        for d in (0, 1):
            if 1 <= s <= steps[d]:
                lad_z_in(d, s - 1).wait_recv()
            if s < steps[d]:
                lad_z(d, s).start()

    lad_step(0)

    @pl.loop(0, part.shape[0])
    def _(j):
        part[j] = jnp.dot(camp_ref[...], cint_ref[j], preferred_element_type=F32)

    for s in (1, 2):
        lad_step(s)
    stage_a(0)
    for s in range(3, steps[0] + 1):
        lad_step(s)
    mine_t2.wait()
    mine_lad.wait()

    codes[y] = code_ref[...]
    for d in (1, 2, 3):
        code_in(d).wait_recv()
    per_y = t2_ref.shape[1]
    lanes = code_ref.shape[1]
    dests = sel.shape[0]
    want = (lax.broadcasted_iota(jnp.int32, (dests, lanes), 0) + y * dests).astype(F32)
    lane = lax.broadcasted_iota(jnp.int32, (1, lanes), 1)
    for h in range(NY * per_y // lanes):
        row = jnp.where(lane < per_y, codes[2 * h, 0:1], codes[2 * h + 1, 0:1])
        sel[:, h * lanes:(h + 1) * lanes] = jnp.where(want == row, 1.0, 0.0).astype(BF)

    def stage_b(c):
        for d in (0, 1):
            fwd_y_in(c, d).wait_recv()

        @pl.loop(0, cr // 4)
        def _(i):
            for u in range(4):
                r = c * cr + i * 4 + u
                tiles = gath[r].reshape(NY * per_y, gath.shape[3])
                got = jnp.dot(sel[...], tiles, preferred_element_type=F32)
                ysum[:, r] = got.astype(BF).reshape(nz, dests // nz, gath.shape[3])

        for d in (0, 1):
            z_copy(c, d, 0).start()

    def z_step(c, s):
        for d in (0, 1):

            @pl.when(s < arm(c, d))
            def _():
                z_copy(c, d, s - 1).wait_recv()
                dest = at_z((1 - 2 * d) * (arm(c, d) - s))
                ysum[dest, chunk(c)] = ysum[dest, chunk(c)] + zin[d, s - 1, chunk(c)]
                z_copy(c, d, s).start()

    def z_last(c):
        total = ysum[z, chunk(c)].astype(F32)
        for d in (0, 1):
            z_copy(c, d, arm(c, d) - 1).wait_recv()
            total = total + zin[d, arm(c, d) - 1, chunk(c)].astype(F32)
        depth = acc.shape[0] // NC
        acc[pl.ds(c * depth, depth)] = total.reshape(depth, acc.shape[1])

    last = nz // 2

    @pl.loop(0, LAG * (NC - 1) + last + 1)
    def _(tick):
        for c in range(NC):
            s = tick - LAG * c
            if c > 0:

                @pl.when(s == -1)
                def _():
                    stage_a(c)
                    if c == NC - 1:
                        for d in (0, 1):
                            lad_y(d, 0).start()

            @pl.when(s == 0)
            def _():
                stage_b(c)

            @pl.when((s > 0) & (s < last))
            def _():
                z_step(c, s)

            @pl.when(s == last)
            def _():
                z_last(c)

            if c == NC - 1:

                @pl.when(s == 3)
                def _():
                    for d in (0, 1):
                        lad_y(d, 2 * d - 1).wait_recv()
                        lad_fwd(d, 2 * d - 1).start()

    for d in (0, 1):
        lad_fwd(d, 2).wait_recv()

    per_owner = ysum.shape[2]
    cds = amps.shape[1] // acc.shape[1]
    blocks = per_owner // (2 * cds)
    for b in range(blocks):
        for h in range(2):
            for cd in range(cds):
                start = (b * cds + cd) * 2 + h
                first = (b * 2 + h) * rows
                amps[first:first + rows, cd * acc.shape[1]:(cd + 1) * acc.shape[1]] = acc[
                    pl.ds(start, rows, stride=per_owner), :
                ].astype(BF)

    def block_of(j):
        per = lgat.shape[0] * nz // (2 * nx)
        first = j * per
        piece_l = lgat[first // nz, pl.ds(first % nz, per)]
        piece_l = piece_l.reshape(per * lgat.shape[2], lgat.shape[3])
        return part[j] + lax.dot_general(
            amps[...], piece_l, (((1,), (1,)), ((), ())), preferred_element_type=F32
        )

    def pair(i):
        return remote(pout.at[i], pin.at[i], ps.at[i], pr.at[i], partner)

    order = (2, 1, 3, 0)
    for n in order:
        i = at_x(n)
        pout[i] = block_of(i * 2 + (1 - core)).astype(BF)
        pair(i).start()
    for n in order:
        i = at_x(n)
        part[i * 2 + core] = block_of(i * 2 + core)

    mid = xs.shape[1] // 2

    def summed(n):
        i = at_x(n)
        pair(i).wait_recv()
        return part[i * 2 + core] + pin[i].astype(F32)

    def far(d):
        return remote(
            xs.at[2, pl.ds(d * mid, mid)], xh.at[d], xsend.at[d], xrecv.at[d], to_x(1 - 2 * d)
        )

    def near(d):
        return remote(xs.at[d], xi.at[d], xsend.at[2 + d], xrecv.at[2 + d], to_x(1 - 2 * d))

    xs[2] = summed(2).astype(BF)
    for d in (0, 1):
        far(d).start()
    for d in (0, 1):
        part[at_x(1 - 2 * d) * 2 + core] = summed(1 - 2 * d)
    part[x * 2 + core] = summed(0)
    for d in (0, 1):
        far(d).wait_recv()
        j = at_x(1 - 2 * d) * 2 + core
        both = part[j, pl.ds(d * mid, mid)] + xh[d].astype(F32)
        xs[d, pl.ds(d * mid, mid)] = both.astype(BF)
        xs[d, pl.ds((1 - d) * mid, mid)] = part[j, pl.ds((1 - d) * mid, mid)].astype(BF)
        near(d).start()
    for d in (0, 1):
        near(d).wait_recv()
    out_ref[...] = (part[x * 2 + core] + xi[0].astype(F32) + xi[1].astype(F32)).astype(BF)

    for d in (1, 2, 3):
        code_out(d).wait_send()
    for c in range(NC):
        for d in (0, 1):
            own_y(c, d).wait_send()
            fwd_y(c, d).wait_send()
            for s in range(arm(c, d)):
                z_copy(c, d, s).wait_send()
    for d in (0, 1):
        for s in range(steps[d]):
            lad_z(d, s).wait_send()
        lad_y(d, 0).wait_send()
        lad_fwd(d, 2 * d - 1).wait_send()
        far(d).wait_send()
        near(d).wait_send()
    for n in order:
        pair(at_x(n)).wait_send()


def body(n_occ, n_vir, t2_tiles, tile_owner, tile_block, tile_cd, ladder_ints, cycle_amps, cycle_ints):
    nz, nx = n_occ // NY, n_vir // 2
    count, size = t2_tiles.shape[:2]
    pair_rows, _ = cycle_amps.shape
    depth, cols = ladder_ints.shape
    ranks, all_cols = cycle_ints.shape
    blocks, cds = pair_rows // size, depth // size
    combos = blocks * cds
    rows = size // 2
    width = all_cols // n_vir
    per_y, per_owner = count * 2, combos * 2
    tiles = t2_tiles.reshape(count, 2, rows, size).transpose(2, 0, 1, 3).reshape(rows, per_y, size)
    code = tile_owner[:, 0] * combos + tile_block * cds + tile_cd
    code = (code[:, None] * 2 + jnp.arange(2, dtype=jnp.int32)[None, :]).reshape(1, per_y)
    code = jnp.tile(code, (8, 128 // per_y)).astype(F32)
    ints = cycle_ints.reshape(ranks, n_vir, width).transpose(1, 0, 2)
    vmem, dma = pltpu.VMEM, pltpu.SemaphoreType.DMA
    near = nz // 2
    return pl.pallas_call(
        kernel,
        out_shape=jax.ShapeDtypeStruct((pair_rows, width), BF),
        in_specs=[pl.BlockSpec(memory_space=vmem)] * 5,
        out_specs=pl.BlockSpec(memory_space=vmem),
        scratch_shapes=[
            vmem((rows, NY, per_y, size), BF),
            vmem((NY, 8, 128), F32),
            vmem((nz * per_owner, NY * per_y), BF),
            vmem((nz, rows, per_owner, size), BF),
            vmem((2, near, rows, per_owner, size), BF),
            vmem((NY, nz, cols, depth), BF),
            vmem((n_vir, pair_rows, width), F32),
            vmem((rows * per_owner, size), F32),
            vmem((pair_rows, depth), BF),
            vmem((nx, pair_rows, width), BF),
            vmem((nx, pair_rows, width), BF),
            vmem((3, pair_rows, width), BF),
            vmem((2, pair_rows // 2, width), BF),
            vmem((2, pair_rows, width), BF),
            dma((NC, 4)), dma((NC, 4)),
            dma((3,)), dma((3,)),
            dma((NC, 2, near)), dma((NC, 2, near)),
            dma((2, near)), dma((2, near)),
            dma((4,)), dma((4,)),
            dma((nx,)), dma((nx,)),
            dma((4,)), dma((4,)),
            dma((2,)),
        ],
        compiler_params=pltpu.CompilerParams(collective_id=0, has_side_effects=True),
    )(tiles, code, ladder_ints.T, cycle_amps, ints)


def solution(mesh):
    in_specs = (
        P(("occ", "vir"), None, None),
        P(("occ", "vir"), None),
        P(("occ", "vir")),
        P(("occ", "vir")),
        P("vir", "occ"),
        P("occ", "vir"),
        P("vir", None),
    )
    return jax.shard_map(
        functools.partial(body, mesh.shape["occ"], mesh.shape["vir"]),
        mesh=mesh, in_specs=in_specs, out_specs=P("occ", "vir"), check_vma=False,
    )
```

```python
import functools

import jax
import jax.numpy as jnp
from jax import lax
from jax.experimental import pallas as pl
from jax.experimental.pallas import tpu as pltpu
from jax.sharding import PartitionSpec as P

MESH = pl.DeviceIdType.MESH
NY = 4
NC = 4
LAD_TICK = 9
EARLY = 5
PASS = (0, 0, 2, 3)
BEGIN = (0, 3, 4, 5)
BF = jnp.bfloat16
F32 = jnp.float32


def kernel(
    t2_ref, code_ref, lad_ref, camp_ref, cint_ref, out_ref,
    gath, codes, sel, ysum, zin, lgat, part, acc, amps, pout, pin, xs, xh, xi,
    ysend, yrecv, csend, crecv, zsend, zrecv, lzs, lzr, lys, lyr, ps, pr, xsend, xrecv, local,
):
    nz = lgat.shape[1]
    rows = t2_ref.shape[0]
    cr = rows // NC
    half = cr // 2
    nx = pout.shape[0]
    occ, vir = lax.axis_index("occ"), lax.axis_index("vir")
    y, z = occ // nz, occ % nz
    x, core = vir // 2, vir % 2

    def at_y(d):
        return (y + d + NY) % NY

    def at_z(d):
        return (z + d + nz) % nz

    def at_x(d):
        return (x + d + nx) % nx

    def to_y(d):
        return {"occ": at_y(d) * nz + z}

    def to_z(d):
        return {"occ": y * nz + at_z(d)}

    def to_x(d):
        return {"vir": at_x(d) * 2 + core}

    partner = {"vir": x * 2 + (1 - core)}

    def remote(src, dst, send, recv, where):
        return pltpu.make_async_remote_copy(
            src_ref=src, dst_ref=dst, send_sem=send, recv_sem=recv, device_id=where,
            device_id_type=MESH,
        )

    def chunk(c):
        return pl.ds(c * cr, cr)

    def own_y(c, d):
        return remote(
            t2_ref.at[chunk(c)], gath.at[chunk(c), y], ysend.at[c, d], yrecv.at[c, d],
            to_y(1 - 2 * d),
        )

    def own_y_in(c, d):
        return remote(
            t2_ref.at[chunk(c)], gath.at[chunk(c), at_y(2 * d - 1)], ysend.at[c, d],
            yrecv.at[c, d], to_y(1 - 2 * d),
        )

    def piece(c, d):
        return pl.ds(c * cr + d * half, half)

    def fwd_y(c, d):
        block = gath.at[piece(c, d), at_y(2 * d - 1)]
        return remote(block, block, ysend.at[c, 2 + d], yrecv.at[c, 2 + d], to_y(1 - 2 * d))

    def fwd_y_in(c, d):
        block = gath.at[piece(c, d), at_y(2)]
        return remote(block, block, ysend.at[c, 2 + d], yrecv.at[c, 2 + d], to_y(1 - 2 * d))

    def code_out(d):
        return remote(code_ref, codes.at[y], csend.at[d - 1], crecv.at[d - 1], to_y(d))

    def code_in(d):
        return remote(code_ref, codes.at[at_y(-d)], csend.at[d - 1], crecv.at[d - 1], to_y(d))

    def arm(c, d):
        return nz // 2 if (c + d) % 2 == 0 else nz - 1 - nz // 2

    def z_copy(c, d, s):
        block = ysum.at[at_z((1 - 2 * d) * (arm(c, d) - s)), chunk(c)]
        return remote(
            block, zin.at[d, s, chunk(c)], zsend.at[c, d, s], zrecv.at[c, d, s], to_z(1 - 2 * d)
        )

    steps = (nz // 2, nz - 1 - nz // 2)

    def lad_z(d, s):
        block = lgat.at[y, at_z((2 * d - 1) * s)]
        src = lad_ref if s == 0 else block
        return remote(src, block, lzs.at[d, s], lzr.at[d, s], to_z(1 - 2 * d))

    def lad_z_in(d, s):
        block = lgat.at[y, at_z((2 * d - 1) * (s + 1))]
        return remote(block, block, lzs.at[d, s], lzr.at[d, s], to_z(1 - 2 * d))

    def lad_y(d, source):
        block = lgat.at[at_y(source)]
        return remote(block, block, lys.at[d], lyr.at[d], to_y(1 - 2 * d))

    def lad_fwd(d, source):
        block = lgat.at[at_y(source), pl.ds(d * (nz // 2), nz // 2)]
        return remote(block, block, lys.at[2 + d], lyr.at[2 + d], to_y(1 - 2 * d))

    barrier = pltpu.get_barrier_semaphore()
    peers = [to_y(1), to_y(2), to_y(-1), to_z(1), to_z(-1), to_x(1), to_x(-1), partner]
    for peer in peers:
        pl.semaphore_signal(barrier, inc=1, device_id=peer, device_id_type=MESH)
    pl.semaphore_wait(barrier, len(peers))

    for d in (1, 2, 3):
        code_out(d).start()
    for d in (0, 1):
        own_y(0, d).start()
    mine_t2 = pltpu.make_async_copy(t2_ref, gath.at[:, y], local.at[0])
    mine_lad = pltpu.make_async_copy(lad_ref, lgat.at[y, z], local.at[1])
    mine_t2.start()
    mine_lad.start()

    def stage_a(c):
        for d in (0, 1):
            own_y_in(c, d).wait_recv()
            fwd_y(c, d).start()
        for n in (1, 2) if c == 0 else (c + 2,):
            if n < NC:
                for d in (0, 1):
                    own_y(n, d).start()

    def lad_step(s):
        for d in (0, 1):
            if 1 <= s <= steps[d]:
                lad_z_in(d, s - 1).wait_recv()
            if s < steps[d]:
                lad_z(d, s).start()

    lad_step(0)

    width = part.shape[2]

    @pl.loop(0, part.shape[0])
    def _(j):
        part[j] = jnp.dot(
            camp_ref[...], cint_ref[:, pl.ds(pl.multiple_of(j * width, width), width)],
            preferred_element_type=F32,
        )

    for s in (1, 2):
        lad_step(s)
    stage_a(0)
    for s in range(3, EARLY):
        lad_step(s)
    mine_t2.wait()
    mine_lad.wait()

    codes[y] = code_ref[...]
    for d in (1, 2, 3):
        code_in(d).wait_recv()
    per_y = t2_ref.shape[1]
    lanes = code_ref.shape[1]
    dests = sel.shape[0]
    want = (lax.broadcasted_iota(jnp.int32, (dests, lanes), 0) + y * dests).astype(F32)
    lane = lax.broadcasted_iota(jnp.int32, (1, lanes), 1)
    for h in range(NY * per_y // lanes):
        row = jnp.where(lane < per_y, codes[2 * h, 0:1], codes[2 * h + 1, 0:1])
        sel[:, h * lanes:(h + 1) * lanes] = jnp.where(want == row, 1.0, 0.0).astype(BF)

    def stage_b(c):
        for d in (0, 1):
            fwd_y_in(c, d).wait_recv()

        @pl.loop(0, cr // 4)
        def _(i):
            size = gath.shape[3]
            for u in (0, 2):
                r = c * cr + i * 4 + u
                tiles = jnp.concatenate(
                    [gath[r + e].reshape(NY * per_y, size) for e in (0, 1)], axis=1
                )
                got = jnp.dot(sel[...], tiles, preferred_element_type=F32).astype(BF)
                for e in (0, 1):
                    ysum[:, r + e] = got[:, e * size:(e + 1) * size].reshape(
                        nz, dests // nz, size
                    )

        for d in (0, 1):
            z_copy(c, d, 0).start()

    def z_step(c, s):
        for d in (0, 1):

            @pl.when(s < arm(c, d))
            def _():
                z_copy(c, d, s - 1).wait_recv()
                dest = at_z((1 - 2 * d) * (arm(c, d) - s))
                ysum[dest, chunk(c)] = ysum[dest, chunk(c)] + zin[d, s - 1, chunk(c)]
                z_copy(c, d, s).start()

    def z_last(c):
        total = ysum[z, chunk(c)].astype(F32)
        for d in (0, 1):
            z_copy(c, d, arm(c, d) - 1).wait_recv()
            total = total + zin[d, arm(c, d) - 1, chunk(c)].astype(F32)
        depth = acc.shape[0] // NC
        acc[pl.ds(c * depth, depth)] = total.reshape(depth, acc.shape[1])

    last = nz // 2

    @pl.loop(0, BEGIN[-1] + last + 1)
    def _(tick):
        for c in range(NC):
            s = tick - BEGIN[c]
            if c > 0:

                @pl.when(tick == PASS[c])
                def _():
                    stage_a(c)

            @pl.when(s == 0)
            def _():
                stage_b(c)

            @pl.when((s > 0) & (s < last))
            def _():
                z_step(c, s)

            @pl.when(s == last)
            def _():
                z_last(c)

        for n in range(EARLY, steps[0] + 1):

            @pl.when(tick == n - EARLY)
            def _():
                lad_step(n)
                if n == steps[0]:
                    for d in (0, 1):
                        lad_y(d, 0).start()

        @pl.when(tick == LAD_TICK)
        def _():
            for d in (0, 1):
                lad_y(d, 2 * d - 1).wait_recv()
                lad_fwd(d, 2 * d - 1).start()

    for d in (0, 1):
        lad_fwd(d, 2).wait_recv()

    per_owner = ysum.shape[2]
    cds = amps.shape[1] // acc.shape[1]
    blocks = per_owner // (2 * cds)
    for b in range(blocks):
        for h in range(2):
            for cd in range(cds):
                start = (b * cds + cd) * 2 + h
                first = (b * 2 + h) * rows
                amps[first:first + rows, cd * acc.shape[1]:(cd + 1) * acc.shape[1]] = acc[
                    pl.ds(start, rows, stride=per_owner), :
                ].astype(BF)

    def block_of(j):
        per = lgat.shape[0] * nz // (2 * nx)
        first = j * per
        piece_l = lgat[first // nz, pl.ds(first % nz, per)]
        piece_l = piece_l.reshape(per * lgat.shape[2], lgat.shape[3])
        return part[j] + lax.dot_general(
            amps[...], piece_l, (((1,), (1,)), ((), ())), preferred_element_type=F32
        )

    def pair(i):
        return remote(pout.at[i], pin.at[i], ps.at[i], pr.at[i], partner)

    order = (2, 1, 3, 0)
    for n in order:
        i = at_x(n)
        pout[i] = block_of(i * 2 + (1 - core)).astype(BF)
        pair(i).start()
    for n in order:
        i = at_x(n)
        part[i * 2 + core] = block_of(i * 2 + core)

    mid = xs.shape[1] // 2

    def summed(n):
        i = at_x(n)
        pair(i).wait_recv()
        return part[i * 2 + core] + pin[i].astype(F32)

    def far(d):
        return remote(
            xs.at[2, pl.ds(d * mid, mid)], xh.at[d], xsend.at[d], xrecv.at[d], to_x(1 - 2 * d)
        )

    def near(d):
        return remote(xs.at[d], xi.at[d], xsend.at[2 + d], xrecv.at[2 + d], to_x(1 - 2 * d))

    xs[2] = summed(2).astype(BF)
    for d in (0, 1):
        far(d).start()
    for d in (0, 1):
        part[at_x(1 - 2 * d) * 2 + core] = summed(1 - 2 * d)
    part[x * 2 + core] = summed(0)
    for d in (0, 1):
        far(d).wait_recv()
        j = at_x(1 - 2 * d) * 2 + core
        both = part[j, pl.ds(d * mid, mid)] + xh[d].astype(F32)
        xs[d, pl.ds(d * mid, mid)] = both.astype(BF)
        xs[d, pl.ds((1 - d) * mid, mid)] = part[j, pl.ds((1 - d) * mid, mid)].astype(BF)
        near(d).start()
    for d in (0, 1):
        near(d).wait_recv()
    out_ref[...] = (part[x * 2 + core] + xi[0].astype(F32) + xi[1].astype(F32)).astype(BF)

    for d in (1, 2, 3):
        code_out(d).wait_send()
    for c in range(NC):
        for d in (0, 1):
            own_y(c, d).wait_send()
            fwd_y(c, d).wait_send()
            for s in range(arm(c, d)):
                z_copy(c, d, s).wait_send()
    for d in (0, 1):
        for s in range(steps[d]):
            lad_z(d, s).wait_send()
        lad_y(d, 0).wait_send()
        lad_fwd(d, 2 * d - 1).wait_send()
        far(d).wait_send()
        near(d).wait_send()
    for n in order:
        pair(at_x(n)).wait_send()


def body(n_occ, n_vir, t2_tiles, tile_owner, tile_block, tile_cd, ladder_ints, cycle_amps, cycle_ints):
    nz, nx = n_occ // NY, n_vir // 2
    count, size = t2_tiles.shape[:2]
    pair_rows, _ = cycle_amps.shape
    depth, cols = ladder_ints.shape
    ranks, all_cols = cycle_ints.shape
    blocks, cds = pair_rows // size, depth // size
    combos = blocks * cds
    rows = size // 2
    width = all_cols // n_vir
    per_y, per_owner = count * 2, combos * 2
    tiles = t2_tiles.reshape(count, 2, rows, size).transpose(2, 0, 1, 3).reshape(rows, per_y, size)
    code = tile_owner[:, 0] * combos + tile_block * cds + tile_cd
    code = (code[:, None] * 2 + jnp.arange(2, dtype=jnp.int32)[None, :]).reshape(1, per_y)
    code = jnp.tile(code, (8, 128 // per_y)).astype(F32)
    vmem, dma = pltpu.VMEM, pltpu.SemaphoreType.DMA
    near = nz // 2
    return pl.pallas_call(
        kernel,
        out_shape=jax.ShapeDtypeStruct((pair_rows, width), BF),
        in_specs=[pl.BlockSpec(memory_space=vmem)] * 5,
        out_specs=pl.BlockSpec(memory_space=vmem),
        scratch_shapes=[
            vmem((rows, NY, per_y, size), BF),
            vmem((NY, 8, 128), F32),
            vmem((nz * per_owner, NY * per_y), BF),
            vmem((nz, rows, per_owner, size), BF),
            vmem((2, near, rows, per_owner, size), BF),
            vmem((NY, nz, cols, depth), BF),
            vmem((n_vir, pair_rows, width), F32),
            vmem((rows * per_owner, size), F32),
            vmem((pair_rows, depth), BF),
            vmem((nx, pair_rows, width), BF),
            vmem((nx, pair_rows, width), BF),
            vmem((3, pair_rows, width), BF),
            vmem((2, pair_rows // 2, width), BF),
            vmem((2, pair_rows, width), BF),
            dma((NC, 4)), dma((NC, 4)),
            dma((3,)), dma((3,)),
            dma((NC, 2, near)), dma((NC, 2, near)),
            dma((2, near)), dma((2, near)),
            dma((4,)), dma((4,)),
            dma((nx,)), dma((nx,)),
            dma((4,)), dma((4,)),
            dma((2,)),
        ],
        compiler_params=pltpu.CompilerParams(collective_id=0, has_side_effects=True),
    )(tiles, code, ladder_ints.T, cycle_amps, cycle_ints)


def solution(mesh):
    in_specs = (
        P(("occ", "vir"), None, None),
        P(("occ", "vir"), None),
        P(("occ", "vir")),
        P(("occ", "vir")),
        P("vir", "occ"),
        P("occ", "vir"),
        P("vir", None),
    )
    return jax.shard_map(
        functools.partial(body, mesh.shape["occ"], mesh.shape["vir"]),
        mesh=mesh, in_specs=in_specs, out_specs=P("occ", "vir"), check_vma=False,
    )
```

```python
import functools

import jax
import jax.numpy as jnp
from jax import lax
from jax.experimental import pallas as pl
from jax.experimental.pallas import tpu as pltpu
from jax.sharding import PartitionSpec as P

MESH = pl.DeviceIdType.MESH
NY = 4
NC = 4
SHARE = (5, 4, 4, 3)
LAD_TICK = 9
EARLY = 5
PASS = (0, 0, 2, 3)
BEGIN = (0, 3, 4, 5)
BF = jnp.bfloat16
F32 = jnp.float32


def kernel(
    t2_ref, code_ref, lad_ref, camp_ref, cint_ref, out_ref,
    gath, codes, sel, ysum, zin, lgat, part, acc, amps, pout, pin, xs, xh, xi,
    ysend, yrecv, csend, crecv, zsend, zrecv, lzs, lzr, lys, lyr, ps, pr, xsend, xrecv, local,
):
    nz = lgat.shape[1]
    rows = t2_ref.shape[0]
    sizes = [rows * n // 16 for n in SHARE]
    starts = [sum(sizes[:c]) for c in range(NC)]
    nx = pout.shape[0]
    occ, vir = lax.axis_index("occ"), lax.axis_index("vir")
    y, z = occ // nz, occ % nz
    x, core = vir // 2, vir % 2

    def at_y(d):
        return (y + d + NY) % NY

    def at_z(d):
        return (z + d + nz) % nz

    def at_x(d):
        return (x + d + nx) % nx

    def to_y(d):
        return {"occ": at_y(d) * nz + z}

    def to_z(d):
        return {"occ": y * nz + at_z(d)}

    def to_x(d):
        return {"vir": at_x(d) * 2 + core}

    partner = {"vir": x * 2 + (1 - core)}

    def remote(src, dst, send, recv, where):
        return pltpu.make_async_remote_copy(
            src_ref=src, dst_ref=dst, send_sem=send, recv_sem=recv, device_id=where,
            device_id_type=MESH,
        )

    def chunk(c):
        return pl.ds(starts[c], sizes[c])

    def own_y(c, d):
        return remote(
            t2_ref.at[chunk(c)], gath.at[y, chunk(c)], ysend.at[c, d], yrecv.at[c, d],
            to_y(1 - 2 * d),
        )

    def own_y_in(c, d):
        return remote(
            t2_ref.at[chunk(c)], gath.at[at_y(2 * d - 1), chunk(c)], ysend.at[c, d],
            yrecv.at[c, d], to_y(1 - 2 * d),
        )

    def piece(c, d):
        half = sizes[c] // 2
        return pl.ds(starts[c] + d * half, half)

    def fwd_y(c, d):
        block = gath.at[at_y(2 * d - 1), piece(c, d)]
        return remote(block, block, ysend.at[c, 2 + d], yrecv.at[c, 2 + d], to_y(1 - 2 * d))

    def fwd_y_in(c, d):
        block = gath.at[at_y(2), piece(c, d)]
        return remote(block, block, ysend.at[c, 2 + d], yrecv.at[c, 2 + d], to_y(1 - 2 * d))

    def code_out(d):
        return remote(code_ref, codes.at[y], csend.at[d - 1], crecv.at[d - 1], to_y(d))

    def code_in(d):
        return remote(code_ref, codes.at[at_y(-d)], csend.at[d - 1], crecv.at[d - 1], to_y(d))

    def arm(c, d):
        return nz // 2 if (c + d) % 2 == 0 else nz - 1 - nz // 2

    def z_copy(c, d, s):
        block = ysum.at[at_z((1 - 2 * d) * (arm(c, d) - s)), chunk(c)]
        return remote(
            block, zin.at[d, s, chunk(c)], zsend.at[c, d, s], zrecv.at[c, d, s], to_z(1 - 2 * d)
        )

    steps = (nz // 2, nz - 1 - nz // 2)

    def lad_z(d, s):
        block = lgat.at[y, at_z((2 * d - 1) * s)]
        src = lad_ref if s == 0 else block
        return remote(src, block, lzs.at[d, s], lzr.at[d, s], to_z(1 - 2 * d))

    def lad_z_in(d, s):
        block = lgat.at[y, at_z((2 * d - 1) * (s + 1))]
        return remote(block, block, lzs.at[d, s], lzr.at[d, s], to_z(1 - 2 * d))

    def lad_y(d, source):
        block = lgat.at[at_y(source)]
        return remote(block, block, lys.at[d], lyr.at[d], to_y(1 - 2 * d))

    def lad_fwd(d, source):
        block = lgat.at[at_y(source), pl.ds(d * (nz // 2), nz // 2)]
        return remote(block, block, lys.at[2 + d], lyr.at[2 + d], to_y(1 - 2 * d))

    barrier = pltpu.get_barrier_semaphore()
    peers = [to_y(1), to_y(2), to_y(-1), to_z(1), to_z(-1), to_x(1), to_x(-1), partner]
    for peer in peers:
        pl.semaphore_signal(barrier, inc=1, device_id=peer, device_id_type=MESH)
    pl.semaphore_wait(barrier, len(peers))

    for d in (1, 2, 3):
        code_out(d).start()
    for d in (0, 1):
        own_y(0, d).start()
    mine_lad = pltpu.make_async_copy(lad_ref, lgat.at[y, z], local.at[0])
    mine_lad.start()

    def stage_a(c):
        for d in (0, 1):
            own_y_in(c, d).wait_recv()
            fwd_y(c, d).start()
        for n in (1, 2) if c == 0 else (c + 2,):
            if n < NC:
                for d in (0, 1):
                    own_y(n, d).start()

    def lad_step(s):
        for d in (0, 1):
            if 1 <= s <= steps[d]:
                lad_z_in(d, s - 1).wait_recv()
            if s < steps[d]:
                lad_z(d, s).start()

    lad_step(0)

    width = part.shape[2]

    @pl.loop(0, rows)
    def _(r):
        gath[y, r] = t2_ref[r]

    @pl.loop(0, part.shape[0])
    def _(j):
        part[j] = jnp.dot(
            camp_ref[...], cint_ref[:, pl.ds(pl.multiple_of(j * width, width), width)],
            preferred_element_type=F32,
        )

    for s in (1, 2):
        lad_step(s)
    stage_a(0)
    for s in range(3, EARLY):
        lad_step(s)
    mine_lad.wait()

    codes[y] = code_ref[...]
    for d in (1, 2, 3):
        code_in(d).wait_recv()
    per_y = t2_ref.shape[1]
    lanes = code_ref.shape[1]
    dests = sel.shape[0]
    want = (lax.broadcasted_iota(jnp.int32, (dests, lanes), 0) + y * dests).astype(F32)
    lane = lax.broadcasted_iota(jnp.int32, (1, lanes), 1)
    for h in range(NY * per_y // lanes):
        row = jnp.where(lane < per_y, codes[2 * h, 0:1], codes[2 * h + 1, 0:1])
        sel[:, h * lanes:(h + 1) * lanes] = jnp.where(want == row, 1.0, 0.0).astype(BF)

    def stage_b(c):
        for d in (0, 1):
            fwd_y_in(c, d).wait_recv()

        @pl.loop(0, sizes[c] // 4)
        def _(i):
            size = gath.shape[3]
            for u in (0, 2):
                r = starts[c] + i * 4 + u
                tiles = jnp.concatenate(
                    [
                        jnp.concatenate([gath[n, r + e] for n in range(NY)], axis=0)
                        for e in (0, 1)
                    ],
                    axis=1,
                )
                got = jnp.dot(sel[...], tiles, preferred_element_type=F32).astype(BF)
                for e in (0, 1):
                    ysum[:, r + e] = got[:, e * size:(e + 1) * size].reshape(
                        nz, dests // nz, size
                    )

        for d in (0, 1):
            z_copy(c, d, 0).start()

    def z_step(c, s):
        for d in (0, 1):

            @pl.when(s < arm(c, d))
            def _():
                z_copy(c, d, s - 1).wait_recv()
                dest = at_z((1 - 2 * d) * (arm(c, d) - s))
                ysum[dest, chunk(c)] = ysum[dest, chunk(c)] + zin[d, s - 1, chunk(c)]
                z_copy(c, d, s).start()

    def z_last(c):
        total = ysum[z, chunk(c)].astype(F32)
        for d in (0, 1):
            z_copy(c, d, arm(c, d) - 1).wait_recv()
            total = total + zin[d, arm(c, d) - 1, chunk(c)].astype(F32)
        per = acc.shape[0] // rows
        acc[pl.ds(starts[c] * per, sizes[c] * per)] = total.reshape(
            sizes[c] * per, acc.shape[1]
        )

    last = nz // 2

    @pl.loop(0, BEGIN[-1] + last + 1)
    def _(tick):
        for c in range(NC):
            s = tick - BEGIN[c]
            if c > 0:

                @pl.when(tick == PASS[c])
                def _():
                    stage_a(c)

            @pl.when(s == 0)
            def _():
                stage_b(c)

            @pl.when((s > 0) & (s < last))
            def _():
                z_step(c, s)

            @pl.when(s == last)
            def _():
                z_last(c)

        for n in range(EARLY, steps[0] + 1):

            @pl.when(tick == n - EARLY)
            def _():
                lad_step(n)
                if n == steps[0]:
                    for d in (0, 1):
                        lad_y(d, 0).start()

        @pl.when(tick == LAD_TICK)
        def _():
            for d in (0, 1):
                lad_y(d, 2 * d - 1).wait_recv()
                lad_fwd(d, 2 * d - 1).start()

    for d in (0, 1):
        lad_fwd(d, 2).wait_recv()

    per_owner = ysum.shape[2]
    cds = amps.shape[1] // acc.shape[1]
    blocks = per_owner // (2 * cds)
    for b in range(blocks):
        for h in range(2):
            for cd in range(cds):
                start = (b * cds + cd) * 2 + h
                first = (b * 2 + h) * rows
                amps[first:first + rows, cd * acc.shape[1]:(cd + 1) * acc.shape[1]] = acc[
                    pl.ds(start, rows, stride=per_owner), :
                ].astype(BF)

    def block_of(j):
        per = lgat.shape[0] * nz // (2 * nx)
        first = j * per
        piece_l = lgat[first // nz, pl.ds(first % nz, per)]
        piece_l = piece_l.reshape(per * lgat.shape[2], lgat.shape[3])
        return part[j] + lax.dot_general(
            amps[...], piece_l, (((1,), (1,)), ((), ())), preferred_element_type=F32
        )

    def pair(i):
        return remote(pout.at[i], pin.at[i], ps.at[i], pr.at[i], partner)

    order = (2, 1, 3, 0)
    for n in order:
        i = at_x(n)
        pout[i] = block_of(i * 2 + (1 - core)).astype(BF)
        pair(i).start()
    for n in order:
        i = at_x(n)
        part[i * 2 + core] = block_of(i * 2 + core)

    mid = xs.shape[1] // 2

    def summed(n):
        i = at_x(n)
        pair(i).wait_recv()
        return part[i * 2 + core] + pin[i].astype(F32)

    def far(d):
        return remote(
            xs.at[2, pl.ds(d * mid, mid)], xh.at[d], xsend.at[d], xrecv.at[d], to_x(1 - 2 * d)
        )

    def near(d):
        return remote(xs.at[d], xi.at[d], xsend.at[2 + d], xrecv.at[2 + d], to_x(1 - 2 * d))

    xs[2] = summed(2).astype(BF)
    for d in (0, 1):
        far(d).start()
    for d in (0, 1):
        part[at_x(1 - 2 * d) * 2 + core] = summed(1 - 2 * d)
    part[x * 2 + core] = summed(0)
    for d in (0, 1):
        far(d).wait_recv()
        j = at_x(1 - 2 * d) * 2 + core
        both = part[j, pl.ds(d * mid, mid)] + xh[d].astype(F32)
        xs[d, pl.ds(d * mid, mid)] = both.astype(BF)
        xs[d, pl.ds((1 - d) * mid, mid)] = part[j, pl.ds((1 - d) * mid, mid)].astype(BF)
        near(d).start()
    for d in (0, 1):
        near(d).wait_recv()
    out_ref[...] = (part[x * 2 + core] + xi[0].astype(F32) + xi[1].astype(F32)).astype(BF)

    for d in (1, 2, 3):
        code_out(d).wait_send()
    for c in range(NC):
        for d in (0, 1):
            own_y(c, d).wait_send()
            fwd_y(c, d).wait_send()
            for s in range(arm(c, d)):
                z_copy(c, d, s).wait_send()
    for d in (0, 1):
        for s in range(steps[d]):
            lad_z(d, s).wait_send()
        lad_y(d, 0).wait_send()
        lad_fwd(d, 2 * d - 1).wait_send()
        far(d).wait_send()
        near(d).wait_send()
    for n in order:
        pair(at_x(n)).wait_send()


def body(n_occ, n_vir, t2_tiles, tile_owner, tile_block, tile_cd, ladder_ints, cycle_amps, cycle_ints):
    nz, nx = n_occ // NY, n_vir // 2
    count, size = t2_tiles.shape[:2]
    pair_rows, _ = cycle_amps.shape
    depth, cols = ladder_ints.shape
    ranks, all_cols = cycle_ints.shape
    blocks, cds = pair_rows // size, depth // size
    combos = blocks * cds
    rows = size // 2
    width = all_cols // n_vir
    per_y, per_owner = count * 2, combos * 2
    tiles = t2_tiles.reshape(count, 2, rows, size).transpose(2, 0, 1, 3).reshape(rows, per_y, size)
    code = tile_owner[:, 0] * combos + tile_block * cds + tile_cd
    code = (code[:, None] * 2 + jnp.arange(2, dtype=jnp.int32)[None, :]).reshape(1, per_y)
    code = jnp.tile(code, (8, 128 // per_y)).astype(F32)
    vmem, dma = pltpu.VMEM, pltpu.SemaphoreType.DMA
    near = nz // 2
    return pl.pallas_call(
        kernel,
        out_shape=jax.ShapeDtypeStruct((pair_rows, width), BF),
        in_specs=[pl.BlockSpec(memory_space=vmem)] * 5,
        out_specs=pl.BlockSpec(memory_space=vmem),
        scratch_shapes=[
            vmem((NY, rows, per_y, size), BF),
            vmem((NY, 8, 128), F32),
            vmem((nz * per_owner, NY * per_y), BF),
            vmem((nz, rows, per_owner, size), BF),
            vmem((2, near, rows, per_owner, size), BF),
            vmem((NY, nz, cols, depth), BF),
            vmem((n_vir, pair_rows, width), F32),
            vmem((rows * per_owner, size), F32),
            vmem((pair_rows, depth), BF),
            vmem((nx, pair_rows, width), BF),
            vmem((nx, pair_rows, width), BF),
            vmem((3, pair_rows, width), BF),
            vmem((2, pair_rows // 2, width), BF),
            vmem((2, pair_rows, width), BF),
            dma((NC, 4)), dma((NC, 4)),
            dma((3,)), dma((3,)),
            dma((NC, 2, near)), dma((NC, 2, near)),
            dma((2, near)), dma((2, near)),
            dma((4,)), dma((4,)),
            dma((nx,)), dma((nx,)),
            dma((4,)), dma((4,)),
            dma((1,)),
        ],
        compiler_params=pltpu.CompilerParams(collective_id=0, has_side_effects=True),
    )(tiles, code, ladder_ints.T, cycle_amps, cycle_ints)


def solution(mesh):
    in_specs = (
        P(("occ", "vir"), None, None),
        P(("occ", "vir"), None),
        P(("occ", "vir")),
        P(("occ", "vir")),
        P("vir", "occ"),
        P("occ", "vir"),
        P("vir", None),
    )
    return jax.shard_map(
        functools.partial(body, mesh.shape["occ"], mesh.shape["vir"]),
        mesh=mesh, in_specs=in_specs, out_specs=P("occ", "vir"), check_vma=False,
    )
```
